256 devices in a mesh: sweep: 4 (over y), xsec: 64 (over x, z, core).
Axes of the slice: x: 4, y: 4, z: 8, core: 2. Of those that a mesh axis runs over, the one named last changes fastest.
Arguments:
- cond_block: bfloat16 [4, 64, 2, 24, 40, 512], P('sweep', 'xsec'), may hold values from -0.15625 to 0.15625
- interior_src: bfloat16 [4, 64, 2, 4, 40, 512], P('sweep', 'xsec'), may hold values from -6 to 6
- face_index: int32 [4, 64, 64, 192], P('sweep', 'xsec'), may hold values from 0 to 255
- owner_count: int32 [4, 64, 64], P('sweep', 'xsec'), may hold values from 1 to 8, as said below
- coupling: float32 [8, 2, 8192], P('sweep', None, 'xsec'), may hold values from -1 to 1
- schur_inv: bfloat16 [8, 2, 8192, 8192], P('sweep', None, None, 'xsec'), may hold values from -0.046875 to 0.046875
Outputs:
- sweep_sol: float32 [8, 8, 8192], P('sweep', None, 'xsec')
The draws below stay inside these ranges and needn't reach their ends.
Inputs may be any that keep to these rules, and one draw needn't show every extreme that they name: `owner_count`: every count is at least 1 and at most 8; in each sweep row some owner receives 8 live slots from every sender.
All inputs are finite; a program needn't handle non-finite values.
Results may differ from the reference program's by a relative error of at most 0.006.
Values may be sent and summed in bfloat16 or wider, within the bound.
A program may use at most 64 MiB of HBM per device.

```python
import jax
import jax.numpy as jnp
from jax import lax

NT = 24
NI = 40
SRC = 4
LAY_DEV = 2
TR_DEV = 128
CAP = 8
LAYERS = 8
TRACE = 8192
ELEMS = 512
FACES = 192
SLOTS = 256
N_SWEEP = 4
N_XSEC = 64


def draw_owner_count(key, part):
    key_base, key_hot = jax.random.split(jax.random.fold_in(key, 17))
    base = jax.random.randint(key_base, (N_SWEEP, N_XSEC, N_XSEC), 1, CAP // 2 + 1)
    hottest = jax.random.randint(key_hot, (N_SWEEP, 1, 1), 0, N_XSEC)
    owners = jnp.arange(N_XSEC)[None, :, None]
    return jnp.where(owners == hottest, CAP, base).astype(jnp.int32)


def place_ends(array, key, smallest, top_value):
    longest = array.shape.index(max(array.shape))
    spots = []
    for shift in (0, 1):
        where = [jax.random.randint(jax.random.fold_in(key, axis), (), 0, length) for axis, length in enumerate(array.shape)]
        where[longest] = (where[longest] + shift) % array.shape[longest]
        spots.append(tuple(where))
    return array.at[spots[0]].set(smallest).at[spots[1]].set(top_value)


def levels(rng, dims, shards, least, largest):
    def one(dim, parts):
        draws = jax.random.uniform(jax.random.fold_in(jax.random.fold_in(rng, 6), dim), (parts,), jnp.float32, least / len(shards), largest / len(shards))
        return jnp.repeat(jnp.exp(draws), dims[dim] // parts).reshape((-1,) + (1,) * (len(dims) - dim - 1))

    gain = one(*shards[0])
    for cut in shards[1:]:
        gain = gain * one(*cut)
    return gain


def noise(stream_key, shape, scale, limit, cuts=(), kind=jnp.bfloat16):
    drawn = scale * jax.random.normal(stream_key, shape, jnp.float32)
    if cuts:
        drawn = drawn * levels(stream_key, shape, cuts, -0.22, 0.18)
    return jnp.clip(drawn, -limit, limit).astype(kind)


def setup_inputs(seed: int = 0) -> dict:
    key_list = jax.random.split(jax.random.key(seed), 7)
    return {
        "cond_block": noise(key_list[0], (N_SWEEP, N_XSEC, 2, NT, NI, ELEMS), (32 * NI) ** -0.5, 0.15625, ((0, 4), (1, 64))),
        "interior_src": noise(key_list[1], (N_SWEEP, N_XSEC, 2, SRC, NI, ELEMS), 1.0, 6.0, ((0, 4), (1, 64))),
        "face_index": place_ends(jax.random.randint(key_list[2], (N_SWEEP, N_XSEC, N_XSEC, FACES), 0, SLOTS), jax.random.fold_in(key_list[2], 1), 0, SLOTS - 1).astype(jnp.int32),
        "owner_count": draw_owner_count(jax.random.fold_in(key_list[6], 71), 0),
        "coupling": jnp.clip(jax.random.uniform(key_list[4], (LAYERS, 2, TRACE), jnp.float32, -1.0, 1.0) * levels(key_list[4], (LAYERS, 2, TRACE), ((0, 4), (2, 64)), -0.4, 0.0), -1.0, 1.0),
        "schur_inv": noise(key_list[5], (LAYERS, 2, TRACE, TRACE), (2 * TRACE) ** -0.5, 0.046875, ((0, 4), (3, 64))),
    }


def condense(blocks, interior):
    left = blocks.astype(jnp.float32).reshape(N_XSEC, 2, NT, NI, N_XSEC, CAP)
    right = interior.astype(jnp.float32).reshape(N_XSEC, 2, SRC, NI, N_XSEC, CAP)

    def contract(first, second):
        return jnp.einsum("ckidp,csidp->dcskp", first, second, precision=lax.Precision.HIGHEST)

    real_part = contract(left[:, 0], right[:, 0]) - contract(left[:, 1], right[:, 1])
    imag_part = contract(left[:, 0], right[:, 1]) + contract(left[:, 1], right[:, 0])
    return jnp.stack([real_part, imag_part], 2).reshape(N_XSEC, N_XSEC, 2 * SRC, FACES)


def assemble_row(packed):
    blocks, interior, index_row, count_row = packed
    values = condense(blocks, interior)
    positions = (jnp.arange(FACES) % CAP).astype(jnp.int32)
    live_mask = positions[None, None, :] < count_row[:, :, None]
    values = jnp.where(live_mask[:, :, None, :], values, jnp.float32(0.0))
    owners = (jnp.arange(N_XSEC) * SLOTS).astype(jnp.int32)
    seg_ids = (index_row + owners[:, None, None]).astype(jnp.int32)
    flat_values = jnp.moveaxis(values, 2, 3).reshape(-1, 2 * SRC)
    summed = jax.ops.segment_sum(flat_values, seg_ids.reshape(-1), num_segments=N_XSEC * SLOTS)
    summed = summed.reshape(N_XSEC, LAY_DEV, TR_DEV, 2 * SRC)
    return summed.transpose(1, 3, 0, 2).reshape(LAY_DEV, 2 * SRC, TRACE)


def reference(cond_block, interior_src, face_index, owner_count, coupling, schur_inv):
    loads = lax.map(assemble_row, (cond_block, interior_src, face_index, owner_count))
    loads = loads.reshape(LAYERS, 2 * SRC, TRACE)
    carried = jnp.zeros((2, SRC, TRACE), jnp.float32)
    outputs = []
    for layer_at in range(LAYERS):
        layer_loads = loads[layer_at].reshape(2, SRC, TRACE)
        couple = coupling[layer_at]
        real_part = layer_loads[0] - (couple[0] * carried[0] - couple[1] * carried[1])
        imag_part = layer_loads[1] - (couple[0] * carried[1] + couple[1] * carried[0])
        rhs = jnp.concatenate([real_part, imag_part], 0).astype(jnp.bfloat16)
        first = jnp.dot(rhs, schur_inv[layer_at, 0], preferred_element_type=jnp.float32)
        second = jnp.dot(rhs, schur_inv[layer_at, 1], preferred_element_type=jnp.float32)
        carried = jnp.stack([first[:SRC] - second[SRC:], second[:SRC] + first[SRC:]], 0)
        outputs.append(carried.reshape(2 * SRC, TRACE))
    return jnp.stack(outputs, 0)
```

```python
import functools

import jax
import jax.numpy as jnp
from jax import lax
from jax.experimental import pallas as pl
from jax.experimental.pallas import tpu as pltpu
from jax.sharding import PartitionSpec as P

CAP = 8
MESH = pl.DeviceIdType.MESH
NX, NZ = 4, 8
DX_ORDER = (2, 1, 3, 0)
DZ_ORDER = (4, 3, 5, 2, 6, 1, 7, 0)


def peers_far_first():
    offsets = [(dx, dz, dc) for dx in range(NX) for dz in range(NZ) for dc in range(2)]
    offsets.remove((0, 0, 0))
    return sorted(offsets, key=lambda o: -(min(o[0], NX - o[0]) + min(o[1], NZ - o[1])))


def row_iota(shape):
    return lax.broadcasted_iota(jnp.int32, shape, 0)


def lane_iota(shape):
    return lax.broadcasted_iota(jnp.int32, shape, 1)


def sum_rows(parts):
    rows = row_iota((8, 128))
    top = rows < 4
    level = [
        jnp.where(top, parts[m], parts[m + 4])
        + pltpu.roll(jnp.where(top, parts[m + 4], parts[m]), 4, 0)
        for m in range(4)
    ]
    for step in (2, 1):
        low = (rows & step) == 0
        level = [
            jnp.where(
                low,
                level[m] + pltpu.roll(level[m], 8 - step, 0),
                level[m + step] + pltpu.roll(level[m + step], step, 0),
            )
            for m in range(step)
        ]
    return level[0]


def swap_groups(values, steps):
    groups = lane_iota((8, 128)) // CAP
    values = list(values)
    for step in steps:
        upper = (groups & step) != 0
        for at in range(len(values)):
            if at & step:
                continue
            first, second = values[at], values[at + step]
            values[at] = jnp.where(upper, pltpu.roll(second, step * CAP, 1), first)
            values[at + step] = jnp.where(upper, second, pltpu.roll(first, 128 - step * CAP, 1))
    return values


def kernel(
    count, inter, face, coup, cond, schur, out,
    cond_v, schur_v, inter_f, terms, send_v, recv_v, onehot,
    rhs_v, gath_v, u_send, u_recv,
    cond_sem, schur_sem, a2a_send, a2a_recv, rhs_send, rhs_recv, usend_sem, urecv_sem,
):
    me = lax.axis_index("xsec")
    row = lax.axis_index("sweep")
    mx, mz, mc = me // 16, (me // 2) % 8, me % 2
    n_faces = cond.shape[1]
    layers = schur.shape[0]

    def tile_of(dx):
        return (mx + dx) % NX

    def peer(offset):
        dx, dz, dc = offset
        return tile_of(dx) * 16 + ((mz + dz) % NZ) * 2 + (mc + dc) % 2

    def lanes_of(dx):
        return pl.ds(pl.multiple_of(tile_of(dx) * 128, 128), 128)

    cond_copies = [
        pltpu.make_async_copy(
            cond.at[:, :, :, lanes_of(dx)], cond_v.at[:, :, :, lanes_of(dx)], cond_sem.at[at]
        )
        for at, dx in enumerate(DX_ORDER)
    ]
    for copy in cond_copies:
        copy.start()
    schur_copies = [
        pltpu.make_async_copy(schur.at[layer], schur_v.at[layer], schur_sem.at[layer])
        for layer in range(layers)
    ]
    for copy in schur_copies:
        copy.start()

    order = peers_far_first()
    barrier = pltpu.get_barrier_semaphore()
    for offset in order:
        pl.semaphore_signal(barrier, inc=1, device_id=(row, peer(offset)), device_id_type=MESH)
    pl.semaphore_signal(barrier, inc=1, device_id=((row + 1) % 4, me), device_id_type=MESH)
    pl.semaphore_signal(barrier, inc=1, device_id=((row + 3) % 4, me), device_id_type=MESH)

    for at, dx in enumerate(DX_ORDER):
        lanes = lanes_of(dx)
        inter_f[...] = inter[:, :, :, lanes].astype(jnp.float32)
        cond_copies[at].wait()

        def one_face(k, carry):
            real = cond_v[0, k, :, lanes].astype(jnp.float32)
            imag = cond_v[1, k, :, lanes].astype(jnp.float32)

            def fold(value):
                return sum(value[8 * v : 8 * v + 8] for v in range(value.shape[0] // 8))

            real_parts = [fold(real * inter_f[0, j] - imag * inter_f[1, j]) for j in range(4)]
            imag_parts = [fold(real * inter_f[1, j] + imag * inter_f[0, j]) for j in range(4)]
            terms[k] = sum_rows(real_parts + imag_parts)
            return carry

        lax.fori_loop(0, n_faces, one_face, 0, unroll=4)
        first = swap_groups([terms[k] for k in range(16)], (8, 4, 2, 1))
        second = swap_groups([terms[k] for k in range(16, 24)], (4, 2, 1))
        base = tile_of(dx) * 16
        for d in range(16):
            tail = second[d % 8] if d < 8 else pltpu.roll(second[d % 8], 64, 1)
            send_v[base + d] = jnp.concatenate([first[d], tail], 1).astype(jnp.bfloat16)
        if at == 0:
            pl.semaphore_wait(barrier, len(order) + 2)
        for dz in DZ_ORDER:
            for dc in range(2):
                if (dx, dz, dc) == (0, 0, 0):
                    continue
                target = peer((dx, dz, dc))
                pltpu.make_async_remote_copy(
                    src_ref=send_v.at[target], dst_ref=recv_v.at[me],
                    send_sem=a2a_send, recv_sem=a2a_recv,
                    device_id=(row, target), device_id_type=MESH,
                ).start()
    recv_v[me] = send_v[me]

    slots = onehot.shape[1]
    columns = lane_iota((1, 256))
    place = columns % CAP
    unknown = row_iota((slots, 256))

    def one_sender(c, carry):
        index = jnp.concatenate([face[pl.ds(c, 1), :], jnp.full((1, 64), -1, jnp.int32)], 1)
        index = jnp.where(place < count[0, c], index, -1)
        onehot[c] = jnp.where(unknown == index, 1.0, 0.0).astype(jnp.bfloat16)
        return carry

    senders = recv_v.shape[0]
    lax.fori_loop(0, senders, one_sender, 0)

    others = pl.ds(0, senders - 1)
    pltpu.make_async_copy(recv_v.at[others], recv_v.at[others], a2a_recv).wait()

    def add_sender(c, total):
        return total + lax.dot_general(
            recv_v[c], onehot[c], (((1,), (1,)), ((), ())), preferred_element_type=jnp.float32
        )

    loads = lax.fori_loop(0, senders, add_sender, jnp.zeros((8, slots), jnp.float32), unroll=8)

    sign = jnp.where(row_iota((8, 128)) < 4, -1.0, 1.0)

    def turned(value):
        return sign * pltpu.roll(value, 4, 0)

    @pl.when(row == 0)
    def _():
        u_recv[...] = jnp.zeros_like(u_recv)

    @pl.when(row > 0)
    def _():
        pltpu.make_async_copy(u_recv, u_recv, urecv_sem).wait()

    u = u_recv[...]
    for layer in range(layers):
        load = loads[:, layer * 128 : (layer + 1) * 128]
        rhs = load - (coup[layer, 0:1, :] * u + coup[layer, 1:2, :] * turned(u))
        rhs_v[layer] = rhs.astype(jnp.bfloat16)
        for offset in order:
            pltpu.make_async_remote_copy(
                src_ref=rhs_v.at[layer], dst_ref=gath_v.at[layer, me],
                send_sem=rhs_send.at[layer], recv_sem=rhs_recv.at[layer],
                device_id=(row, peer(offset)), device_id_type=MESH,
            ).start()
        gath_v[layer, me] = rhs_v[layer]
        schur_copies[layer].wait()
        pltpu.make_async_copy(
            gath_v.at[layer, others], gath_v.at[layer, others], rhs_recv.at[layer]
        ).wait()

        def add_chip(chip, total):
            left = jnp.concatenate([gath_v[layer, 2 * chip], gath_v[layer, 2 * chip + 1]], 1)
            rows = pl.ds(pl.multiple_of(chip * 256, 256), 256)
            right = jnp.concatenate([schur_v[layer, 0, rows, :], schur_v[layer, 1, rows, :]], 1)
            return total + jnp.dot(left, right, preferred_element_type=jnp.float32)

        total = lax.fori_loop(0, senders // 2, add_chip, jnp.zeros((8, 256), jnp.float32), unroll=8)
        u = total[:, :128] + turned(total[:, 128:])
        out[layer] = u

    @pl.when(row < 3)
    def _():
        u_send[...] = u
        copy = pltpu.make_async_remote_copy(
            src_ref=u_send, dst_ref=u_recv, send_sem=usend_sem, recv_sem=urecv_sem,
            device_id=(row + 1, me), device_id_type=MESH,
        )
        copy.start()
        copy.wait_send()

    pltpu.make_async_copy(send_v.at[others], send_v.at[others], a2a_send).wait()
    for layer in range(layers):
        pltpu.make_async_copy(
            gath_v.at[layer, others], gath_v.at[layer, others], rhs_send.at[layer]
        ).wait()


def shards(cond_block, interior_src, face_index, owner_count, coupling, schur_inv):
    cond, inter = cond_block[0, 0], interior_src[0, 0]
    face, count = face_index[0, 0], owner_count[0]
    layers, _, trace, width = schur_inv.shape
    peers = face.shape[0]
    vmem = pl.BlockSpec(memory_space=pltpu.VMEM)
    hbm = pl.BlockSpec(memory_space=pl.ANY)
    f32, bf16 = jnp.float32, jnp.bfloat16
    dma = pltpu.SemaphoreType.DMA
    return pl.pallas_call(
        kernel,
        out_shape=jax.ShapeDtypeStruct((layers, 8, width), f32),
        in_specs=[pl.BlockSpec(memory_space=pltpu.SMEM), vmem, vmem, vmem, hbm, hbm],
        out_specs=vmem,
        scratch_shapes=[
            pltpu.VMEM(cond.shape, bf16),
            pltpu.VMEM(schur_inv.shape, bf16),
            pltpu.VMEM((*inter.shape[:3], 128), f32),
            pltpu.VMEM((cond.shape[1], 8, 128), f32),
            pltpu.VMEM((peers, 8, 256), bf16),
            pltpu.VMEM((peers, 8, 256), bf16),
            pltpu.VMEM((peers, layers * width, 256), bf16),
            pltpu.VMEM((layers, 8, width), bf16),
            pltpu.VMEM((layers, peers, 8, width), bf16),
            pltpu.VMEM((8, width), f32),
            pltpu.VMEM((8, width), f32),
            dma((4,)), dma((layers,)), dma, dma, dma((layers,)), dma((layers,)), dma, dma,
        ],
        compiler_params=pltpu.CompilerParams(
            collective_id=0, has_side_effects=True, vmem_limit_bytes=60 << 20
        ),
    )(count, inter, face, coupling, cond, schur_inv)


def solution(mesh):
    placed = (
        P("sweep", "xsec", None, None, None, None),
        P("sweep", "xsec", None, None, None, None),
        P("sweep", "xsec", None, None),
        P("sweep", "xsec", None),
        P("sweep", None, "xsec"),
        P("sweep", None, None, "xsec"),
    )
    return jax.shard_map(
        shards, mesh=mesh, in_specs=placed, out_specs=P("sweep", None, "xsec"), check_vma=False
    )
```

```python
import functools

import jax
import jax.numpy as jnp
from jax import lax
from jax.experimental import pallas as pl
from jax.experimental.pallas import tpu as pltpu
from jax.sharding import PartitionSpec as P

CAP = 8
MESH = pl.DeviceIdType.MESH
NX, NZ = 4, 8
DX_ORDER = (2, 1, 3, 0)
DZ_ORDER = (4, 3, 5, 2, 6, 1, 7, 0)
BARRIER_AT = 1
NEAR = ((0, 2), (3, 3), (4, 4))
VMEM_BYTES = 60 << 20


def hops(offset):
    return min(offset[0], NX - offset[0]) + min(offset[1], NZ - offset[1])


def chips_by_group():
    chips = sorted(((dx, dz) for dx in range(NX) for dz in range(NZ)), key=hops)
    near = [[o for o in chips if low <= hops(o) <= high] for low, high in NEAR]
    return near, [o for o in chips if hops(o) > NEAR[-1][1]]


def opposite(chip):
    return (-chip[0]) % NX, (-chip[1]) % NZ


def peers_far_first():
    offsets = [(dx, dz, dc) for dx in range(NX) for dz in range(NZ) for dc in range(2)]
    offsets.remove((0, 0, 0))
    return sorted(offsets, key=lambda o: -hops(o))


def row_iota(shape):
    return lax.broadcasted_iota(jnp.int32, shape, 0)


def lane_iota(shape):
    return lax.broadcasted_iota(jnp.int32, shape, 1)


def sum_rows(parts):
    rows = row_iota((8, 128))
    top = rows < 4
    level = [
        jnp.where(top, parts[m], parts[m + 4])
        + pltpu.roll(jnp.where(top, parts[m + 4], parts[m]), 4, 0)
        for m in range(4)
    ]
    for step in (2, 1):
        low = (rows & step) == 0
        level = [
            jnp.where(
                low,
                level[m] + pltpu.roll(level[m], 8 - step, 0),
                level[m + step] + pltpu.roll(level[m + step], step, 0),
            )
            for m in range(step)
        ]
    return level[0]


def swap_groups(values, steps):
    groups = lane_iota((8, 128)) // CAP
    values = list(values)
    for step in steps:
        upper = (groups & step) != 0
        for at in range(len(values)):
            if at & step:
                continue
            first, second = values[at], values[at + step]
            values[at] = jnp.where(upper, pltpu.roll(second, step * CAP, 1), first)
            values[at + step] = jnp.where(upper, second, pltpu.roll(first, 128 - step * CAP, 1))
    return values


def kernel(
    count_h, inter_h, face_h, coup_h, cond, schur, out,
    cond_v, schur_v, inter_v, face_v, count_v, coup_v, inter_f, terms, send_v, recv_v, onehot,
    rhs_v, near_v, pass_v, far_v, ahead_send, ahead_recv,
    in_sem, cond_sem, schur_sem, a2a_send, a2a_recv,
    rhs_send, near_recv, pass_send, pass_recv, far_recv, ahead_send_sem, ahead_recv_sem,
):
    me = lax.axis_index("xsec")
    row = lax.axis_index("sweep")
    mx, mz, mc = me // 16, (me // 2) % 8, me % 2
    n_faces = cond.shape[1]
    layers = schur.shape[0]
    senders = recv_v.shape[0]
    slots = onehot.shape[2]

    def tile_of(dx):
        return (mx + dx) % NX

    def peer(offset):
        dx, dz, dc = offset
        return tile_of(dx) * 16 + ((mz + dz) % NZ) * 2 + (mc + dc) % 2

    def lanes_of(dx):
        return pl.ds(pl.multiple_of(tile_of(dx) * 128, 128), 128)

    small_copies = [
        pltpu.make_async_copy(source, target, in_sem.at[at])
        for at, (source, target) in enumerate(
            ((inter_h, inter_v), (face_h, face_v), (count_h, count_v), (coup_h, coup_v))
        )
    ]
    cond_copies = [
        pltpu.make_async_copy(
            cond.at[:, :, :, lanes_of(dx)], cond_v.at[:, :, :, lanes_of(dx)], cond_sem.at[at]
        )
        for at, dx in enumerate(DX_ORDER)
    ]
    schur_copies = [
        pltpu.make_async_copy(schur.at[layer], schur_v.at[layer], schur_sem.at[layer])
        for layer in range(layers)
    ]
    small_copies[0].start()
    for copy in cond_copies + small_copies[1:] + schur_copies:
        copy.start()

    order = peers_far_first()
    barrier = pltpu.get_barrier_semaphore()
    for offset in order:
        pl.semaphore_signal(barrier, inc=1, device_id=(row, peer(offset)), device_id_type=MESH)
    pl.semaphore_signal(barrier, inc=1, device_id=((row + 1) % 4, me), device_id_type=MESH)
    pl.semaphore_signal(barrier, inc=1, device_id=((row + 3) % 4, me), device_id_type=MESH)

    def send_tile(at):
        dx = DX_ORDER[at]
        for dz in DZ_ORDER:
            for dc in range(2):
                if (dx, dz, dc) == (0, 0, 0):
                    continue
                target = peer((dx, dz, dc))
                pltpu.make_async_remote_copy(
                    src_ref=send_v.at[target], dst_ref=recv_v.at[me],
                    send_sem=a2a_send, recv_sem=a2a_recv.at[at],
                    device_id=(row, target), device_id_type=MESH,
                ).start()

    small_copies[0].wait()
    for at, dx in enumerate(DX_ORDER):
        lanes = lanes_of(dx)
        inter_f[...] = inter_v[:, :, :, lanes].astype(jnp.float32)
        cond_copies[at].wait()

        def one_face(k, carry):
            real = cond_v[0, k, :, lanes].astype(jnp.float32)
            imag = cond_v[1, k, :, lanes].astype(jnp.float32)

            def fold(value):
                return sum(value[8 * v : 8 * v + 8] for v in range(value.shape[0] // 8))

            real_parts = [fold(real * inter_f[0, j] - imag * inter_f[1, j]) for j in range(4)]
            imag_parts = [fold(real * inter_f[1, j] + imag * inter_f[0, j]) for j in range(4)]
            terms[k] = sum_rows(real_parts + imag_parts)
            return carry

        lax.fori_loop(0, n_faces, one_face, 0, unroll=4)
        first = swap_groups([terms[k] for k in range(16)], (8, 4, 2, 1))
        second = swap_groups([terms[k] for k in range(16, 24)], (4, 2, 1))
        base = tile_of(dx) * 16
        left = lane_iota((8, 128)) < 64
        for d in range(16):
            value = second[d % 8]
            if d < 8:
                tail = jnp.where(left, value, pltpu.roll(pltpu.roll(value, 64, 1), 4, 0))
            else:
                tail = jnp.where(left, pltpu.roll(value, 64, 1), pltpu.roll(value, 4, 0))
            send_v[base + d, 0] = first[d][:4].astype(jnp.bfloat16)
            send_v[base + d, 1] = first[d][4:].astype(jnp.bfloat16)
            send_v[base + d, 2] = tail[:4].astype(jnp.bfloat16)
        if at == BARRIER_AT:
            pl.semaphore_wait(barrier, len(order) + 2)
            for earlier in range(at):
                send_tile(earlier)
        if at >= BARRIER_AT:
            send_tile(at)
    recv_v[me] = send_v[me]

    for copy in small_copies[1:]:
        copy.wait()
    n_rows = n_faces * CAP
    index = jnp.concatenate(
        [face_v[...], jnp.zeros((senders, 256 - n_rows), jnp.int32)], 1
    )
    index = jnp.concatenate([index, jnp.zeros((128 - senders, 256), jnp.int32)], 0)
    index = jnp.concatenate([index[:, :128].T, index[:, 128:].T], 0)[:n_rows]
    counts = jnp.concatenate([count_v[...], jnp.zeros((1, 128 - senders), jnp.int32)], 1)
    index = jnp.where(row_iota((n_rows, 128)) % CAP < counts, index, -1)
    index = index.astype(jnp.float32).astype(jnp.bfloat16)
    unknown = lane_iota((n_rows, slots)).astype(jnp.float32).astype(jnp.bfloat16)
    one, zero = jnp.ones((), jnp.bfloat16), jnp.zeros((), jnp.bfloat16)

    for c in range(senders):
        onehot[c] = jnp.where(index[:, c : c + 1] == unknown, one, zero)

    def add_sender(c, total):
        top, bottom, tail = (recv_v[c, part].astype(jnp.float32) for part in range(3))
        head = jnp.concatenate([top, bottom], 0)
        tail = jnp.concatenate([tail[:, :64], tail[:, 64:]], 0)
        block = jnp.concatenate([head, tail], 1).astype(jnp.bfloat16)
        return total + jnp.dot(block, onehot[c], preferred_element_type=jnp.float32)

    loads = jnp.zeros((8, slots), jnp.float32)
    for at, dx in enumerate(DX_ORDER):
        some = recv_v.at[pl.ds(0, 16 if dx else 15)]
        pltpu.make_async_copy(some, some, a2a_recv.at[at]).wait()
        start = tile_of(NX - dx) * 16
        loads = lax.fori_loop(
            0, 16, lambda i, total: add_sender(start + i, total), loads, unroll=8
        )

    sign = jnp.where(row_iota((8, 128)) < 4, -1.0, 1.0)
    groups, far = chips_by_group()
    starts = [sum(len(g) for g in groups[:at]) for at in range(len(groups))]
    near = [chip for group in groups for chip in group]

    def turned(value):
        return sign * pltpu.roll(value, 4, 0)

    def right_side(load, couple, u):
        return load - (couple[0:1] * u + couple[1:2] * turned(u))

    def send_rhs(at, layer, to_row, own):
        source = rhs_v.at[at]

        def start(target, dst, sem):
            pltpu.make_async_remote_copy(
                src_ref=source, dst_ref=dst, send_sem=rhs_send.at[at], recv_sem=sem,
                device_id=(to_row, target), device_id_type=MESH,
            ).start()

        for chip in reversed(far):
            slot = 2 * far.index(opposite(chip)) + mc
            for dc in range(2):
                start(peer((*chip, dc)), far_v.at[layer, slot], far_recv.at[layer])
        for chip in reversed(near):
            slot = near.index(opposite(chip))
            group = max(g for g in range(len(groups)) if starts[g] <= slot)
            if chip != (0, 0) or not own:
                start(peer((*chip, 0)), near_v.at[layer, slot], near_recv.at[layer, group])
        if own:
            pltpu.make_async_copy(source, near_v.at[layer, 0], near_recv.at[layer, 0]).start()

    remote_near, remote_far = len(near) - 1, 2 * len(far)

    def solve(layer):
        partner = peer((0, 0, 1))
        passes = []
        schur_copies[layer].wait()
        total = jnp.zeros((8, 256), jnp.float32)

        def rows_of(chip, core):
            first = (tile_of(chip[0]) * 8 + (mz + chip[1]) % NZ) * 256 + core * 128
            rows = pl.ds(pl.multiple_of(first, 128), 128)
            return jnp.concatenate([schur_v[layer, 0, rows, :], schur_v[layer, 1, rows, :]], 1)

        def add_blocks(total, blocks):
            while len(blocks) >= 2:
                pair, blocks = blocks[:2], blocks[2:]
                left = jnp.concatenate([ref[layer, slot] for ref, slot, _, _ in pair], 1)
                right = jnp.concatenate([rows_of(chip, core) for _, _, chip, core in pair], 0)
                total = total + jnp.dot(left, right, preferred_element_type=jnp.float32)
            return total, blocks

        left_over = []
        for at, group in enumerate(groups):
            part = pl.ds(starts[at], len(group))
            some = near_v.at[layer, part]
            pltpu.make_async_copy(some, some, near_recv.at[layer, at]).wait()
            passes.append(
                pltpu.make_async_remote_copy(
                    src_ref=some, dst_ref=pass_v.at[layer, part],
                    send_sem=pass_send.at[layer, at], recv_sem=pass_recv.at[layer, at],
                    device_id=(row, partner), device_id_type=MESH,
                )
            )
            passes[-1].start()
            blocks = [(near_v, near.index(chip), chip, mc) for chip in group]
            total, left_over = add_blocks(total, left_over + blocks)
        def add_passed(total, left_over, at):
            passes[at].wait_recv()
            blocks = [(pass_v, near.index(chip), chip, 1 - mc) for chip in groups[at]]
            return add_blocks(total, left_over + blocks)

        for at in range(len(groups) - 1):
            total, left_over = add_passed(total, left_over, at)
        some = far_v.at[layer]
        pltpu.make_async_copy(some, some, far_recv.at[layer]).wait()
        blocks = [(far_v, 2 * at + core, chip, core) for at, chip in enumerate(far) for core in (0, 1)]
        total, left_over = add_blocks(total, left_over + blocks)
        total, left_over = add_passed(total, left_over, len(groups) - 1)
        assert not left_over
        u = total[:, :128] + turned(total[:, 128:])
        out[layer] = u
        return u, passes

    ahead_send[0:8, :] = loads[:, :128]
    ahead_send[8:10, :] = coup_v[0]
    ahead = pltpu.make_async_remote_copy(
        src_ref=ahead_send, dst_ref=ahead_recv, send_sem=ahead_send_sem,
        recv_sem=ahead_recv_sem, device_id=(row - 1, me), device_id_type=MESH,
    )

    @pl.when(row > 0)
    def _():
        ahead.start()

    @pl.when(row == 0)
    def _():
        zero = jnp.zeros((8, 128), jnp.float32)
        rhs_v[0] = right_side(loads[:, :128], coup_v[0], zero).astype(jnp.bfloat16)
        send_rhs(0, 0, row, True)

    u, passes_0 = solve(0)
    rhs_v[1] = right_side(loads[:, 128:], coup_v[1], u).astype(jnp.bfloat16)
    send_rhs(1, 1, row, True)
    u, passes_1 = solve(1)

    @pl.when(row < 3)
    def _():
        pltpu.make_async_copy(ahead_recv, ahead_recv, ahead_recv_sem).wait()
        rhs = right_side(ahead_recv[0:8, :], ahead_recv[8:10, :], u)
        rhs_v[2] = rhs.astype(jnp.bfloat16)
        send_rhs(2, 0, row + 1, False)

    others = pl.ds(0, senders - 1)
    pltpu.make_async_copy(send_v.at[others], send_v.at[others], a2a_send).wait()
    for copy in passes_0 + passes_1:
        copy.wait_send()

    def wait_sent(at, count):
        some = near_v.reshape(-1, 8, 128).at[pl.ds(0, count)]
        pltpu.make_async_copy(some, some, rhs_send.at[at]).wait()

    wait_sent(1, remote_near + remote_far)

    @pl.when(row > 0)
    def _():
        ahead.wait_send()

    @pl.when(row == 0)
    def _():
        wait_sent(0, remote_near + remote_far)

    @pl.when(row < 3)
    def _():
        wait_sent(2, remote_near + 1 + remote_far)


def shards(cond_block, interior_src, face_index, owner_count, coupling, schur_inv):
    cond, inter = cond_block[0, 0], interior_src[0, 0]
    face, count = face_index[0, 0], owner_count[0]
    layers, _, trace, width = schur_inv.shape
    peers = face.shape[0]
    near, far = (sum(map(len, chips_by_group()[0])), len(chips_by_group()[1]))
    vmem = pl.BlockSpec(memory_space=pltpu.VMEM)
    hbm = pl.BlockSpec(memory_space=pl.ANY)
    f32, bf16 = jnp.float32, jnp.bfloat16
    dma = pltpu.SemaphoreType.DMA
    return pl.pallas_call(
        kernel,
        out_shape=jax.ShapeDtypeStruct((layers, 8, width), f32),
        in_specs=[hbm] * 6,
        out_specs=vmem,
        scratch_shapes=[
            pltpu.VMEM(cond.shape, bf16),
            pltpu.VMEM(schur_inv.shape, bf16),
            pltpu.VMEM(inter.shape, bf16),
            pltpu.VMEM(face.shape, jnp.int32),
            pltpu.VMEM(count.shape, jnp.int32),
            pltpu.VMEM(coupling.shape, f32),
            pltpu.VMEM((*inter.shape[:3], 128), f32),
            pltpu.VMEM((cond.shape[1], 8, 128), f32),
            pltpu.VMEM((peers, 3, 4, 128), bf16),
            pltpu.VMEM((peers, 3, 4, 128), bf16),
            pltpu.VMEM((peers, face.shape[1], layers * width), bf16),
            pltpu.VMEM((layers + 1, 8, width), bf16),
            pltpu.VMEM((layers, near, 8, width), bf16),
            pltpu.VMEM((layers, near, 8, width), bf16),
            pltpu.VMEM((layers, 2 * far, 8, width), bf16),
            pltpu.VMEM((10, width), f32),
            pltpu.VMEM((10, width), f32),
            dma((4,)), dma((4,)), dma((layers,)), dma, dma((4,)),
            dma((layers + 1,)), dma((layers, len(NEAR))), dma((layers, len(NEAR))),
            dma((layers, len(NEAR))), dma((layers,)), dma, dma,
        ],
        compiler_params=pltpu.CompilerParams(
            collective_id=0, has_side_effects=True, vmem_limit_bytes=VMEM_BYTES
        ),
    )(count, inter, face, coupling, cond, schur_inv)


def solution(mesh):
    placed = (
        P("sweep", "xsec", None, None, None, None),
        P("sweep", "xsec", None, None, None, None),
        P("sweep", "xsec", None, None),
        P("sweep", "xsec", None),
        P("sweep", None, "xsec"),
        P("sweep", None, None, "xsec"),
    )
    return jax.shard_map(
        shards, mesh=mesh, in_specs=placed, out_specs=P("sweep", None, "xsec"), check_vma=False
    )
```

```python
import functools

import jax
import jax.numpy as jnp
from jax import lax
from jax.experimental import pallas as pl
from jax.experimental.pallas import tpu as pltpu
from jax.sharding import PartitionSpec as P

CAP = 8
MESH = pl.DeviceIdType.MESH
NX, NZ = 4, 8
DX_ORDER = (2, 1, 3, 0)
DZ_ORDER = (4, 3, 5, 2, 6, 1, 7, 0)
BARRIER_AT = 1
NEAR = ((0, 2), (3, 3), (4, 4))
VMEM_BYTES = 60 << 20


def hops(offset):
    return min(offset[0], NX - offset[0]) + min(offset[1], NZ - offset[1])


def chips_by_group():
    chips = sorted(((dx, dz) for dx in range(NX) for dz in range(NZ)), key=hops)
    near = [[o for o in chips if low <= hops(o) <= high] for low, high in NEAR]
    return near, [o for o in chips if hops(o) > NEAR[-1][1]]


def opposite(chip):
    return (-chip[0]) % NX, (-chip[1]) % NZ


def peers_far_first():
    offsets = [(dx, dz, dc) for dx in range(NX) for dz in range(NZ) for dc in range(2)]
    offsets.remove((0, 0, 0))
    return sorted(offsets, key=lambda o: -hops(o))


def row_iota(shape):
    return lax.broadcasted_iota(jnp.int32, shape, 0)


def lane_iota(shape):
    return lax.broadcasted_iota(jnp.int32, shape, 1)


def sum_rows(parts):
    rows = row_iota((8, 128))
    top = rows < 4
    level = [
        jnp.where(top, parts[m], parts[m + 4])
        + pltpu.roll(jnp.where(top, parts[m + 4], parts[m]), 4, 0)
        for m in range(4)
    ]
    for step in (2, 1):
        low = (rows & step) == 0
        level = [
            jnp.where(
                low,
                level[m] + pltpu.roll(level[m], 8 - step, 0),
                level[m + step] + pltpu.roll(level[m + step], step, 0),
            )
            for m in range(step)
        ]
    return level[0]


def swap_groups(values, steps):
    groups = lane_iota((8, 128)) // CAP
    values = list(values)
    for step in steps:
        upper = (groups & step) != 0
        for at in range(len(values)):
            if at & step:
                continue
            first, second = values[at], values[at + step]
            values[at] = jnp.where(upper, pltpu.roll(second, step * CAP, 1), first)
            values[at + step] = jnp.where(upper, second, pltpu.roll(first, 128 - step * CAP, 1))
    return values


def kernel(
    count_h, inter_h, face_h, coup_h, cond, schur, out,
    cond_v, schur_v, inter_v, face_v, count_v, coup_v, inter_f, terms, send_v, recv_v, onehot,
    rhs_v, near_v, pass_v, far_v, stage_v, u_v,
    in_sem, cond_sem, schur_sem, a2a_send, a2a_recv,
    rhs_send, near_recv, pass_send, pass_recv, far_recv, ahead_send_sem, ahead_recv_sem,
):
    me = lax.axis_index("xsec")
    row = lax.axis_index("sweep")
    mx, mz, mc = me // 16, (me // 2) % 8, me % 2
    n_faces = cond.shape[1]
    layers = schur.shape[0]
    senders = recv_v.shape[0]
    slots = onehot.shape[2]

    def tile_of(dx):
        return (mx + dx) % NX

    def peer(offset):
        dx, dz, dc = offset
        return tile_of(dx) * 16 + ((mz + dz) % NZ) * 2 + (mc + dc) % 2

    def lanes_of(dx):
        return pl.ds(pl.multiple_of(tile_of(dx) * 128, 128), 128)

    small_copies = [
        pltpu.make_async_copy(source, target, in_sem.at[at])
        for at, (source, target) in enumerate(
            ((inter_h, inter_v), (face_h, face_v), (count_h, count_v), (coup_h, coup_v))
        )
    ]
    cond_copies = [
        pltpu.make_async_copy(
            cond.at[:, :, :, lanes_of(dx)], cond_v.at[:, :, :, lanes_of(dx)], cond_sem.at[at]
        )
        for at, dx in enumerate(DX_ORDER)
    ]

    def schur_copy(layer):
        return pltpu.make_async_copy(schur.at[layer], schur_v.at[layer], schur_sem.at[layer])

    small_copies[0].start()
    for copy in cond_copies + small_copies[1:] + [schur_copy(layer) for layer in range(layers)]:
        copy.start()

    order = peers_far_first()
    barrier = pltpu.get_barrier_semaphore()
    for offset in order:
        pl.semaphore_signal(barrier, inc=1, device_id=(row, peer(offset)), device_id_type=MESH)
    pl.semaphore_signal(barrier, inc=1, device_id=((row + 1) % 4, me), device_id_type=MESH)
    pl.semaphore_signal(barrier, inc=1, device_id=((row + 3) % 4, me), device_id_type=MESH)

    def send_tile(at):
        dx = DX_ORDER[at]
        for dz in DZ_ORDER:
            for dc in range(2):
                if (dx, dz, dc) == (0, 0, 0):
                    continue
                target = peer((dx, dz, dc))
                pltpu.make_async_remote_copy(
                    src_ref=send_v.at[target], dst_ref=recv_v.at[me],
                    send_sem=a2a_send, recv_sem=a2a_recv.at[at],
                    device_id=(row, target), device_id_type=MESH,
                ).start()

    small_copies[0].wait()
    for at, dx in enumerate(DX_ORDER):
        lanes = lanes_of(dx)
        inter_f[...] = inter_v[:, :, :, lanes].astype(jnp.float32)
        cond_copies[at].wait()

        def one_face(k, carry):
            real = cond_v[0, k, :, lanes].astype(jnp.float32)
            imag = cond_v[1, k, :, lanes].astype(jnp.float32)

            def fold(value):
                return sum(value[8 * v : 8 * v + 8] for v in range(value.shape[0] // 8))

            real_parts = [fold(real * inter_f[0, j] - imag * inter_f[1, j]) for j in range(4)]
            imag_parts = [fold(real * inter_f[1, j] + imag * inter_f[0, j]) for j in range(4)]
            terms[k] = sum_rows(real_parts + imag_parts)
            return carry

        lax.fori_loop(0, n_faces, one_face, 0, unroll=4)
        first = swap_groups([terms[k] for k in range(16)], (8, 4, 2, 1))
        second = swap_groups([terms[k] for k in range(16, 24)], (4, 2, 1))
        base = tile_of(dx) * 16
        left = lane_iota((8, 128)) < 64
        for d in range(16):
            value = second[d % 8]
            if d < 8:
                tail = jnp.where(left, value, pltpu.roll(pltpu.roll(value, 64, 1), 4, 0))
            else:
                tail = jnp.where(left, pltpu.roll(value, 64, 1), pltpu.roll(value, 4, 0))
            send_v[base + d, 0] = first[d][:4].astype(jnp.bfloat16)
            send_v[base + d, 1] = first[d][4:].astype(jnp.bfloat16)
            send_v[base + d, 2] = tail[:4].astype(jnp.bfloat16)
        if at == BARRIER_AT:
            pl.semaphore_wait(barrier, len(order) + 2)
            for earlier in range(at):
                send_tile(earlier)
        if at >= BARRIER_AT:
            send_tile(at)
    recv_v[me] = send_v[me]

    for copy in small_copies[1:]:
        copy.wait()
    n_rows = n_faces * CAP
    index = jnp.concatenate(
        [face_v[...], jnp.zeros((senders, 256 - n_rows), jnp.int32)], 1
    )
    index = jnp.concatenate([index, jnp.zeros((128 - senders, 256), jnp.int32)], 0)
    index = jnp.concatenate([index[:, :128].T, index[:, 128:].T], 0)[:n_rows]
    counts = jnp.concatenate([count_v[...], jnp.zeros((1, 128 - senders), jnp.int32)], 1)
    index = jnp.where(row_iota((n_rows, 128)) % CAP < counts, index, -1)
    index = index.astype(jnp.float32)
    unknown = lane_iota((n_rows, slots)).astype(jnp.float32).astype(jnp.bfloat16)
    one, zero = jnp.ones((), jnp.bfloat16), jnp.zeros((), jnp.bfloat16)

    def some_senders(at, index):
        for c in range(8):
            column = index[:, c : c + 1].astype(jnp.bfloat16)
            onehot[8 * at + c] = jnp.where(column == unknown, one, zero)
        return pltpu.roll(index, 120, 1)

    lax.fori_loop(0, senders // 8, some_senders, index)

    def add_sender(c, total):
        top, bottom, tail = (recv_v[c, part].astype(jnp.float32) for part in range(3))
        head = jnp.concatenate([top, bottom], 0)
        tail = jnp.concatenate([tail[:, :64], tail[:, 64:]], 0)
        block = jnp.concatenate([head, tail], 1).astype(jnp.bfloat16)
        return total + jnp.dot(block, onehot[c], preferred_element_type=jnp.float32)

    loads = jnp.zeros((8, slots), jnp.float32)
    for at, dx in enumerate(DX_ORDER):
        some = recv_v.at[pl.ds(0, 16 if dx else 15)]
        pltpu.make_async_copy(some, some, a2a_recv.at[at]).wait()
        start = tile_of(NX - dx) * 16
        loads = lax.fori_loop(
            0, 16, lambda i, total: add_sender(start + i, total), loads, unroll=8
        )

    sign = jnp.where(row_iota((8, 128)) < 4, -1.0, 1.0)
    groups, far = chips_by_group()
    starts = [sum(len(g) for g in groups[:at]) for at in range(len(groups))]
    near = [chip for group in groups for chip in group]

    def turned(value):
        return sign * pltpu.roll(value, 4, 0)

    def right_side(load, couple, u):
        return load - (couple[0:1] * u + couple[1:2] * turned(u))

    def send_rhs(stage, layer, to_row, own):
        source = rhs_v.at[stage]

        def start(target, dst, sem):
            pltpu.make_async_remote_copy(
                src_ref=source, dst_ref=dst, send_sem=rhs_send.at[stage], recv_sem=sem,
                device_id=(to_row, target), device_id_type=MESH,
            ).start()

        def send_near(chips):
            for chip in chips:
                slot = near.index(opposite(chip))
                group = max(g for g in range(len(groups)) if starts[g] <= slot)
                start(peer((*chip, 0)), near_v.at[layer, slot], near_recv.at[layer, group])

        send_near(groups[-1])
        for chip in reversed(far):
            slot = 2 * far.index(opposite(chip)) + mc
            for dc in range(2):
                start(peer((*chip, dc)), far_v.at[layer, slot], far_recv.at[layer])
        send_near(near[len(near) - len(groups[-1]) - 1 : 0 : -1])

        @pl.when(own)
        def _():
            pltpu.make_async_copy(source, near_v.at[layer, 0], near_recv.at[layer, 0]).start()

        @pl.when(jnp.logical_not(own))
        def _():
            start(me, near_v.at[layer, 0], near_recv.at[layer, 0])

    def passing(layer, group):
        part = pl.ds(starts[group], len(groups[group]))
        return pltpu.make_async_remote_copy(
            src_ref=near_v.at[layer, part], dst_ref=pass_v.at[layer, part],
            send_sem=pass_send.at[layer, group], recv_sem=pass_recv.at[layer, group],
            device_id=(row, peer((0, 0, 1))), device_id_type=MESH,
        )

    def solve(layer):
        passes = []
        schur_copy(layer).wait()
        total = jnp.zeros((8, 256), jnp.float32)

        def rows_of(chip, core):
            first = (tile_of(chip[0]) * 8 + (mz + chip[1]) % NZ) * 256 + core * 128
            rows = pl.ds(pl.multiple_of(first, 128), 128)
            return jnp.concatenate([schur_v[layer, 0, rows, :], schur_v[layer, 1, rows, :]], 1)

        def add_blocks(total, blocks):
            while len(blocks) >= 2:
                pair, blocks = blocks[:2], blocks[2:]
                left = jnp.concatenate([ref[layer, slot] for ref, slot, _, _ in pair], 1)
                right = jnp.concatenate([rows_of(chip, core) for _, _, chip, core in pair], 0)
                total = total + jnp.dot(left, right, preferred_element_type=jnp.float32)
            return total, blocks

        left_over = []
        for at, group in enumerate(groups):
            part = pl.ds(starts[at], len(group))
            some = near_v.at[layer, part]
            pltpu.make_async_copy(some, some, near_recv.at[layer, at]).wait()
            passes.append(passing(layer, at))
            passes[-1].start()
            blocks = [(near_v, near.index(chip), chip, mc) for chip in group]
            total, left_over = add_blocks(total, left_over + blocks)
        def add_passed(total, left_over, at):
            passes[at].wait_recv()
            blocks = [(pass_v, near.index(chip), chip, 1 - mc) for chip in groups[at]]
            return add_blocks(total, left_over + blocks)

        for at in range(len(groups) - 1):
            total, left_over = add_passed(total, left_over, at)
        some = far_v.at[layer]
        pltpu.make_async_copy(some, some, far_recv.at[layer]).wait()
        blocks = [(far_v, 2 * at + core, chip, core) for at, chip in enumerate(far) for core in (0, 1)]
        total, left_over = add_blocks(total, left_over + blocks)
        total, left_over = add_passed(total, left_over, len(groups) - 1)
        assert not left_over
        u = total[:, :128] + turned(total[:, 128:])
        out[layer] = u
        u_v[...] = u

    for layer in range(layers):
        stage_v[layer, 0:8, :] = loads[:, layer * 128 : (layer + 1) * 128]
        stage_v[layer, 8:10, :] = coup_v[layer]
    ahead = pltpu.make_async_remote_copy(
        src_ref=stage_v.at[0], dst_ref=stage_v.at[layers], send_sem=ahead_send_sem,
        recv_sem=ahead_recv_sem, device_id=(row - 1, me), device_id_type=MESH,
    )

    @pl.when(row > 0)
    def _():
        ahead.start()

    u_v[...] = jnp.zeros_like(u_v)

    def one_stage(stage, carry):
        @pl.when(stage > 0)
        def _():
            solve(stage - 1)

        last = stage == layers

        @pl.when(((stage > 0) | (row == 0)) & (jnp.logical_not(last) | (row < 3)))
        def _():
            @pl.when(last)
            def _():
                pltpu.make_async_copy(stage_v.at[0], stage_v.at[layers], ahead_recv_sem).wait()

            rhs = right_side(stage_v[stage, 0:8, :], stage_v[stage, 8:10, :], u_v[...])
            rhs_v[stage] = rhs.astype(jnp.bfloat16)
            send_rhs(stage, stage % layers, row + stage // layers, jnp.logical_not(last))

        return carry

    lax.fori_loop(0, layers + 1, one_stage, 0)

    others = pl.ds(0, senders - 1)
    pltpu.make_async_copy(send_v.at[others], send_v.at[others], a2a_send).wait()
    for layer in range(layers):
        for group in range(len(groups)):
            passing(layer, group).wait_send()

    def wait_sent(stage, count):
        some = near_v.reshape(-1, 8, 128).at[pl.ds(0, count)]
        pltpu.make_async_copy(some, some, rhs_send.at[stage]).wait()

    remote = len(near) - 1 + 2 * len(far)
    wait_sent(1, remote)

    @pl.when(row > 0)
    def _():
        ahead.wait_send()

    @pl.when(row == 0)
    def _():
        wait_sent(0, remote)

    @pl.when(row < 3)
    def _():
        wait_sent(2, remote + 1)


def shards(cond_block, interior_src, face_index, owner_count, coupling, schur_inv):
    cond, inter = cond_block[0, 0], interior_src[0, 0]
    face, count = face_index[0, 0], owner_count[0]
    layers, _, trace, width = schur_inv.shape
    peers = face.shape[0]
    near, far = (sum(map(len, chips_by_group()[0])), len(chips_by_group()[1]))
    vmem = pl.BlockSpec(memory_space=pltpu.VMEM)
    hbm = pl.BlockSpec(memory_space=pl.ANY)
    f32, bf16 = jnp.float32, jnp.bfloat16
    dma = pltpu.SemaphoreType.DMA
    return pl.pallas_call(
        kernel,
        out_shape=pltpu.VMEM((layers, 8, width), f32),
        in_specs=[hbm] * 6,
        out_specs=vmem,
        scratch_shapes=[
            pltpu.VMEM(cond.shape, bf16),
            pltpu.VMEM(schur_inv.shape, bf16),
            pltpu.VMEM(inter.shape, bf16),
            pltpu.VMEM(face.shape, jnp.int32),
            pltpu.VMEM(count.shape, jnp.int32),
            pltpu.VMEM(coupling.shape, f32),
            pltpu.VMEM((*inter.shape[:3], 128), f32),
            pltpu.VMEM((cond.shape[1], 8, 128), f32),
            pltpu.VMEM((peers, 3, 4, 128), bf16),
            pltpu.VMEM((peers, 3, 4, 128), bf16),
            pltpu.VMEM((peers, face.shape[1], layers * width), bf16),
            pltpu.VMEM((layers + 1, 8, width), bf16),
            pltpu.VMEM((layers, near, 8, width), bf16),
            pltpu.VMEM((layers, near, 8, width), bf16),
            pltpu.VMEM((layers, 2 * far, 8, width), bf16),
            pltpu.VMEM((layers + 1, 10, width), f32),
            pltpu.VMEM((8, width), f32),
            dma((4,)), dma((4,)), dma((layers,)), dma, dma((4,)),
            dma((layers + 1,)), dma((layers, len(NEAR))), dma((layers, len(NEAR))),
            dma((layers, len(NEAR))), dma((layers,)), dma, dma,
        ],
        compiler_params=pltpu.CompilerParams(
            collective_id=0, has_side_effects=True, vmem_limit_bytes=VMEM_BYTES
        ),
    )(count, inter, face, coupling, cond, schur_inv)


def solution(mesh):
    placed = (
        P("sweep", "xsec", None, None, None, None),
        P("sweep", "xsec", None, None, None, None),
        P("sweep", "xsec", None, None),
        P("sweep", "xsec", None),
        P("sweep", None, "xsec"),
        P("sweep", None, None, "xsec"),
    )
    return jax.shard_map(
        shards, mesh=mesh, in_specs=placed, out_specs=P("sweep", None, "xsec"), check_vma=False
    )
```

```python
import functools

import jax
import jax.numpy as jnp
from jax import lax
from jax.experimental import pallas as pl
from jax.experimental.pallas import tpu as pltpu
from jax.sharding import PartitionSpec as P

CAP = 8
MESH = pl.DeviceIdType.MESH
NX, NZ = 4, 8
DX_ORDER = (2, 1, 3, 0)
DZ_ORDER = (4, 3, 5, 2, 6, 1, 7, 0)
BARRIER_AT = 1
NEAR = ((0, 3), (4, 4))
VMEM_BYTES = 60 << 20


def hops(offset):
    return min(offset[0], NX - offset[0]) + min(offset[1], NZ - offset[1])


def chips_by_group():
    chips = sorted(((dx, dz) for dx in range(NX) for dz in range(NZ)), key=hops)
    near = [[o for o in chips if low <= hops(o) <= high] for low, high in NEAR]
    return near, [o for o in chips if hops(o) > NEAR[-1][1]]


def opposite(chip):
    return (-chip[0]) % NX, (-chip[1]) % NZ


def peers_far_first():
    offsets = [(dx, dz, dc) for dx in range(NX) for dz in range(NZ) for dc in range(2)]
    offsets.remove((0, 0, 0))
    return sorted(offsets, key=lambda o: -hops(o))


def row_iota(shape):
    return lax.broadcasted_iota(jnp.int32, shape, 0)


def lane_iota(shape):
    return lax.broadcasted_iota(jnp.int32, shape, 1)


def sum_rows(parts):
    rows = row_iota((8, 128))
    top = rows < 4
    level = [
        jnp.where(top, parts[m], parts[m + 4])
        + pltpu.roll(jnp.where(top, parts[m + 4], parts[m]), 4, 0)
        for m in range(4)
    ]
    for step in (2, 1):
        low = (rows & step) == 0
        level = [
            jnp.where(
                low,
                level[m] + pltpu.roll(level[m], 8 - step, 0),
                level[m + step] + pltpu.roll(level[m + step], step, 0),
            )
            for m in range(step)
        ]
    return level[0]


def swap_groups(values, steps):
    groups = lane_iota((8, 128)) // CAP
    values = list(values)
    for step in steps:
        upper = (groups & step) != 0
        for at in range(len(values)):
            if at & step:
                continue
            first, second = values[at], values[at + step]
            values[at] = jnp.where(upper, pltpu.roll(second, step * CAP, 1), first)
            values[at + step] = jnp.where(upper, second, pltpu.roll(first, 128 - step * CAP, 1))
    return values


def kernel(
    count_h, inter_h, face_h, coup_h, cond, schur, out,
    cond_v, schur_v, inter_v, face_v, count_v, coup_v, inter_f, terms, send_v, recv_v, onehot,
    rhs_v, near_v, pass_v, far_v, stage_v, u_v,
    in_sem, cond_sem, schur_sem, a2a_send, a2a_recv,
    rhs_send, near_recv, pass_send, pass_recv, far_recv, ahead_send_sem, ahead_recv_sem,
):
    me = lax.axis_index("xsec")
    row = lax.axis_index("sweep")
    mx, mz, mc = me // 16, (me // 2) % 8, me % 2
    n_faces = cond.shape[1]
    layers = schur.shape[0]
    senders = recv_v.shape[0]
    slots = onehot.shape[2]

    def tile_of(dx):
        return (mx + dx) % NX

    def peer(offset):
        dx, dz, dc = offset
        return tile_of(dx) * 16 + ((mz + dz) % NZ) * 2 + (mc + dc) % 2

    def lanes_of(dx):
        return pl.ds(pl.multiple_of(tile_of(dx) * 128, 128), 128)

    small_copies = [
        pltpu.make_async_copy(source, target, in_sem.at[at])
        for at, (source, target) in enumerate(
            ((inter_h, inter_v), (face_h, face_v), (count_h, count_v), (coup_h, coup_v))
        )
    ]
    cond_copies = [
        pltpu.make_async_copy(
            cond.at[:, :, :, lanes_of(dx)], cond_v.at[:, :, :, lanes_of(dx)], cond_sem.at[at]
        )
        for at, dx in enumerate(DX_ORDER)
    ]

    def schur_copy(layer):
        return pltpu.make_async_copy(schur.at[layer], schur_v.at[layer], schur_sem.at[layer])

    small_copies[0].start()
    for copy in cond_copies + small_copies[1:] + [schur_copy(layer) for layer in range(layers)]:
        copy.start()

    order = peers_far_first()
    barrier = pltpu.get_barrier_semaphore()
    for offset in order:
        pl.semaphore_signal(barrier, inc=1, device_id=(row, peer(offset)), device_id_type=MESH)
    pl.semaphore_signal(barrier, inc=1, device_id=((row + 1) % 4, me), device_id_type=MESH)
    pl.semaphore_signal(barrier, inc=1, device_id=((row + 3) % 4, me), device_id_type=MESH)

    def send_tile(at):
        dx = DX_ORDER[at]
        for dz in DZ_ORDER:
            for dc in range(2):
                if (dx, dz, dc) == (0, 0, 0):
                    continue
                target = peer((dx, dz, dc))
                pltpu.make_async_remote_copy(
                    src_ref=send_v.at[target], dst_ref=recv_v.at[me],
                    send_sem=a2a_send, recv_sem=a2a_recv.at[at],
                    device_id=(row, target), device_id_type=MESH,
                ).start()

    small_copies[0].wait()
    for at, dx in enumerate(DX_ORDER):
        lanes = lanes_of(dx)
        inter_f[...] = inter_v[:, :, :, lanes].astype(jnp.float32)
        cond_copies[at].wait()

        def one_face(k, carry):
            real = cond_v[0, k, :, lanes].astype(jnp.float32)
            imag = cond_v[1, k, :, lanes].astype(jnp.float32)

            def fold(value):
                return sum(value[8 * v : 8 * v + 8] for v in range(value.shape[0] // 8))

            real_parts = [fold(real * inter_f[0, j] - imag * inter_f[1, j]) for j in range(4)]
            imag_parts = [fold(real * inter_f[1, j] + imag * inter_f[0, j]) for j in range(4)]
            terms[k] = sum_rows(real_parts + imag_parts)
            return carry

        lax.fori_loop(0, n_faces, one_face, 0, unroll=4)
        first = swap_groups([terms[k] for k in range(16)], (8, 4, 2, 1))
        second = swap_groups([terms[k] for k in range(16, 24)], (4, 2, 1))
        base = tile_of(dx) * 16
        left = lane_iota((8, 128)) < 64
        for d in range(16):
            value = second[d % 8]
            if d < 8:
                tail = jnp.where(left, value, pltpu.roll(pltpu.roll(value, 64, 1), 4, 0))
            else:
                tail = jnp.where(left, pltpu.roll(value, 64, 1), pltpu.roll(value, 4, 0))
            send_v[base + d, 0] = first[d][:4].astype(jnp.bfloat16)
            send_v[base + d, 1] = first[d][4:].astype(jnp.bfloat16)
            send_v[base + d, 2] = tail[:4].astype(jnp.bfloat16)
        if at == BARRIER_AT:
            pl.semaphore_wait(barrier, len(order) + 2)
            for earlier in range(at):
                send_tile(earlier)
        if at >= BARRIER_AT:
            send_tile(at)
    recv_v[me] = send_v[me]

    for copy in small_copies[1:]:
        copy.wait()
    n_rows = n_faces * CAP
    index = jnp.concatenate(
        [face_v[...], jnp.zeros((senders, 256 - n_rows), jnp.int32)], 1
    )
    index = jnp.concatenate([index, jnp.zeros((128 - senders, 256), jnp.int32)], 0)
    index = jnp.concatenate([index[:, :128].T, index[:, 128:].T], 0)[:n_rows]
    counts = jnp.concatenate([count_v[...], jnp.zeros((1, 128 - senders), jnp.int32)], 1)
    index = jnp.where(row_iota((n_rows, 128)) % CAP < counts, index, -1)
    index = index.astype(jnp.float32)
    unknown = lane_iota((n_rows, slots)).astype(jnp.float32).astype(jnp.bfloat16)
    one, zero = jnp.ones((), jnp.bfloat16), jnp.zeros((), jnp.bfloat16)

    def some_senders(at, index):
        for c in range(8):
            column = index[:, c : c + 1].astype(jnp.bfloat16)
            onehot[8 * at + c] = jnp.where(column == unknown, one, zero)
        return pltpu.roll(index, 120, 1)

    lax.fori_loop(0, senders // 8, some_senders, index)

    def add_sender(c, total):
        top, bottom, tail = (recv_v[c, part].astype(jnp.float32) for part in range(3))
        head = jnp.concatenate([top, bottom], 0)
        tail = jnp.concatenate([tail[:, :64], tail[:, 64:]], 0)
        block = jnp.concatenate([head, tail], 1).astype(jnp.bfloat16)
        return total + jnp.dot(block, onehot[c], preferred_element_type=jnp.float32)

    loads = jnp.zeros((8, slots), jnp.float32)
    for at, dx in enumerate(DX_ORDER):
        some = recv_v.at[pl.ds(0, 16 if dx else 15)]
        pltpu.make_async_copy(some, some, a2a_recv.at[at]).wait()
        start = tile_of(NX - dx) * 16
        loads = lax.fori_loop(
            0, 16, lambda i, total: add_sender(start + i, total), loads, unroll=8
        )

    sign = jnp.where(row_iota((8, 128)) < 4, -1.0, 1.0)
    groups, far = chips_by_group()
    starts = [sum(len(g) for g in groups[:at]) for at in range(len(groups))]
    near = [chip for group in groups for chip in group]

    def turned(value):
        return sign * pltpu.roll(value, 4, 0)

    def right_side(load, couple, u):
        return load - (couple[0:1] * u + couple[1:2] * turned(u))

    def send_rhs(stage, layer, to_row, own):
        source = rhs_v.at[stage]

        def start(target, dst, sem):
            pltpu.make_async_remote_copy(
                src_ref=source, dst_ref=dst, send_sem=rhs_send.at[stage], recv_sem=sem,
                device_id=(to_row, target), device_id_type=MESH,
            ).start()

        def send_near(chips):
            for chip in chips:
                slot = near.index(opposite(chip))
                group = max(g for g in range(len(groups)) if starts[g] <= slot)
                start(peer((*chip, 0)), near_v.at[layer, slot], near_recv.at[layer, group])

        send_near(groups[-1])
        for chip in reversed(far):
            slot = 2 * far.index(opposite(chip)) + mc
            for dc in range(2):
                start(peer((*chip, dc)), far_v.at[layer, slot], far_recv.at[layer])
        send_near(near[len(near) - len(groups[-1]) - 1 : 0 : -1])

        @pl.when(own)
        def _():
            pltpu.make_async_copy(source, near_v.at[layer, 0], near_recv.at[layer, 0]).start()

        @pl.when(jnp.logical_not(own))
        def _():
            start(me, near_v.at[layer, 0], near_recv.at[layer, 0])

    def passing(layer, group):
        part = pl.ds(starts[group], len(groups[group]))
        return pltpu.make_async_remote_copy(
            src_ref=near_v.at[layer, part], dst_ref=pass_v.at[layer, part],
            send_sem=pass_send.at[layer, group], recv_sem=pass_recv.at[layer, group],
            device_id=(row, peer((0, 0, 1))), device_id_type=MESH,
        )

    def solve(layer):
        passes = []
        schur_copy(layer).wait()
        total = jnp.zeros((8, 256), jnp.float32)

        def rows_of(chip, core):
            first = (tile_of(chip[0]) * 8 + (mz + chip[1]) % NZ) * 256 + core * 128
            rows = pl.ds(pl.multiple_of(first, 128), 128)
            return jnp.concatenate([schur_v[layer, 0, rows, :], schur_v[layer, 1, rows, :]], 1)

        def add_blocks(total, blocks):
            while len(blocks) >= 2:
                pair, blocks = blocks[:2], blocks[2:]
                left = jnp.concatenate([ref[layer, slot] for ref, slot, _, _ in pair], 1)
                right = jnp.concatenate([rows_of(chip, core) for _, _, chip, core in pair], 0)
                total = total + jnp.dot(left, right, preferred_element_type=jnp.float32)
            return total, blocks

        left_over = []
        for at, group in enumerate(groups):
            part = pl.ds(starts[at], len(group))
            some = near_v.at[layer, part]
            pltpu.make_async_copy(some, some, near_recv.at[layer, at]).wait()
            passes.append(passing(layer, at))
            passes[-1].start()
            left_over = left_over + [(near_v, near.index(chip), chip, mc) for chip in group]
        total, left_over = add_blocks(total, left_over)
        def add_passed(total, left_over, at):
            passes[at].wait_recv()
            blocks = [(pass_v, near.index(chip), chip, 1 - mc) for chip in groups[at]]
            return add_blocks(total, left_over + blocks)

        for at in range(len(groups) - 1):
            total, left_over = add_passed(total, left_over, at)
        some = far_v.at[layer]
        pltpu.make_async_copy(some, some, far_recv.at[layer]).wait()
        passes[-1].wait_recv()
        blocks = [(far_v, 2 * at + core, chip, core) for at, chip in enumerate(far) for core in (0, 1)]
        blocks += [(pass_v, near.index(chip), chip, 1 - mc) for chip in groups[-1]]
        total, left_over = add_blocks(total, left_over + blocks)
        assert not left_over
        u = total[:, :128] + turned(total[:, 128:])
        out[layer] = u
        u_v[...] = u

    for layer in range(layers):
        stage_v[layer, 0:8, :] = loads[:, layer * 128 : (layer + 1) * 128]
        stage_v[layer, 8:10, :] = coup_v[layer]
    ahead = pltpu.make_async_remote_copy(
        src_ref=stage_v.at[0], dst_ref=stage_v.at[layers], send_sem=ahead_send_sem,
        recv_sem=ahead_recv_sem, device_id=(row - 1, me), device_id_type=MESH,
    )

    @pl.when(row > 0)
    def _():
        ahead.start()

    u_v[...] = jnp.zeros_like(u_v)

    def one_stage(stage, carry):
        @pl.when(stage > 0)
        def _():
            solve(stage - 1)

        last = stage == layers

        @pl.when(((stage > 0) | (row == 0)) & (jnp.logical_not(last) | (row < 3)))
        def _():
            @pl.when(last)
            def _():
                pltpu.make_async_copy(stage_v.at[0], stage_v.at[layers], ahead_recv_sem).wait()

            rhs = right_side(stage_v[stage, 0:8, :], stage_v[stage, 8:10, :], u_v[...])
            rhs_v[stage] = rhs.astype(jnp.bfloat16)
            send_rhs(stage, stage % layers, row + stage // layers, jnp.logical_not(last))

        return carry

    lax.fori_loop(0, layers + 1, one_stage, 0)

    others = pl.ds(0, senders - 1)
    pltpu.make_async_copy(send_v.at[others], send_v.at[others], a2a_send).wait()
    for layer in range(layers):
        for group in range(len(groups)):
            passing(layer, group).wait_send()

    def wait_sent(stage, count):
        some = near_v.reshape(-1, 8, 128).at[pl.ds(0, count)]
        pltpu.make_async_copy(some, some, rhs_send.at[stage]).wait()

    remote = len(near) - 1 + 2 * len(far)
    wait_sent(1, remote)

    @pl.when(row > 0)
    def _():
        ahead.wait_send()

    @pl.when(row == 0)
    def _():
        wait_sent(0, remote)

    @pl.when(row < 3)
    def _():
        wait_sent(2, remote + 1)


def shards(cond_block, interior_src, face_index, owner_count, coupling, schur_inv):
    cond, inter = cond_block[0, 0], interior_src[0, 0]
    face, count = face_index[0, 0], owner_count[0]
    layers, _, trace, width = schur_inv.shape
    peers = face.shape[0]
    near, far = (sum(map(len, chips_by_group()[0])), len(chips_by_group()[1]))
    vmem = pl.BlockSpec(memory_space=pltpu.VMEM)
    hbm = pl.BlockSpec(memory_space=pl.ANY)
    f32, bf16 = jnp.float32, jnp.bfloat16
    dma = pltpu.SemaphoreType.DMA
    return pl.pallas_call(
        kernel,
        out_shape=pltpu.VMEM((layers, 8, width), f32),
        in_specs=[hbm] * 6,
        out_specs=vmem,
        scratch_shapes=[
            pltpu.VMEM(cond.shape, bf16),
            pltpu.VMEM(schur_inv.shape, bf16),
            pltpu.VMEM(inter.shape, bf16),
            pltpu.VMEM(face.shape, jnp.int32),
            pltpu.VMEM(count.shape, jnp.int32),
            pltpu.VMEM(coupling.shape, f32),
            pltpu.VMEM((*inter.shape[:3], 128), f32),
            pltpu.VMEM((cond.shape[1], 8, 128), f32),
            pltpu.VMEM((peers, 3, 4, 128), bf16),
            pltpu.VMEM((peers, 3, 4, 128), bf16),
            pltpu.VMEM((peers, face.shape[1], layers * width), bf16),
            pltpu.VMEM((layers + 1, 8, width), bf16),
            pltpu.VMEM((layers, near, 8, width), bf16),
            pltpu.VMEM((layers, near, 8, width), bf16),
            pltpu.VMEM((layers, 2 * far, 8, width), bf16),
            pltpu.VMEM((layers + 1, 10, width), f32),
            pltpu.VMEM((8, width), f32),
            dma((4,)), dma((4,)), dma((layers,)), dma, dma((4,)),
            dma((layers + 1,)), dma((layers, len(NEAR))), dma((layers, len(NEAR))),
            dma((layers, len(NEAR))), dma((layers,)), dma, dma,
        ],
        compiler_params=pltpu.CompilerParams(
            collective_id=0, has_side_effects=True, vmem_limit_bytes=VMEM_BYTES
        ),
    )(count, inter, face, coupling, cond, schur_inv)


def solution(mesh):
    placed = (
        P("sweep", "xsec", None, None, None, None),
        P("sweep", "xsec", None, None, None, None),
        P("sweep", "xsec", None, None),
        P("sweep", "xsec", None),
        P("sweep", None, "xsec"),
        P("sweep", None, None, "xsec"),
    )
    return jax.shard_map(
        shards, mesh=mesh, in_specs=placed, out_specs=P("sweep", None, "xsec"), check_vma=False
    )
```

```python
import functools

import jax
import jax.numpy as jnp
from jax import lax
from jax.experimental import pallas as pl
from jax.experimental.pallas import tpu as pltpu
from jax.sharding import PartitionSpec as P

CAP = 8
MESH = pl.DeviceIdType.MESH
NX, NZ = 4, 8
DX_ORDER = (2, 1, 3, 0)
DZ_ORDER = (4, 3, 5, 2, 6, 1, 7, 0)
BARRIER_AT = 1
NEAR = ((0, 3), (4, 4))
VMEM_BYTES = 60 << 20


def hops(offset):
    return min(offset[0], NX - offset[0]) + min(offset[1], NZ - offset[1])


def chips_by_group():
    chips = sorted(((dx, dz) for dx in range(NX) for dz in range(NZ)), key=hops)
    near = [[o for o in chips if low <= hops(o) <= high] for low, high in NEAR]
    return near, [o for o in chips if hops(o) > NEAR[-1][1]]


def opposite(chip):
    return (-chip[0]) % NX, (-chip[1]) % NZ


def peers_far_first():
    offsets = [(dx, dz, dc) for dx in range(NX) for dz in range(NZ) for dc in range(2)]
    offsets.remove((0, 0, 0))
    return sorted(offsets, key=lambda o: -hops(o))


def row_iota(shape):
    return lax.broadcasted_iota(jnp.int32, shape, 0)


def lane_iota(shape):
    return lax.broadcasted_iota(jnp.int32, shape, 1)


def sum_rows(parts):
    rows = row_iota((8, 128))
    top = rows < 4
    level = [
        jnp.where(top, parts[m], parts[m + 4])
        + pltpu.roll(jnp.where(top, parts[m + 4], parts[m]), 4, 0)
        for m in range(4)
    ]
    for step in (2, 1):
        low = (rows & step) == 0
        level = [
            jnp.where(
                low,
                level[m] + pltpu.roll(level[m], 8 - step, 0),
                level[m + step] + pltpu.roll(level[m + step], step, 0),
            )
            for m in range(step)
        ]
    return level[0]


def swap_groups(values, steps):
    groups = lane_iota((8, 128)) // CAP
    values = list(values)
    for step in steps:
        upper = (groups & step) != 0
        for at in range(len(values)):
            if at & step:
                continue
            first, second = values[at], values[at + step]
            values[at] = jnp.where(upper, pltpu.roll(second, step * CAP, 1), first)
            values[at + step] = jnp.where(upper, second, pltpu.roll(first, 128 - step * CAP, 1))
    return values


def kernel(
    count_h, inter_h, face_h, coup_h, cond, schur, out,
    cond_v, schur_v, inter_v, face_v, count_v, coup_v, inter_f, terms, send_v, recv_v, onehot,
    rhs_v, near_v, pass_v, far_v, stage_v, u_v,
    in_sem, cond_sem, schur_sem, a2a_send, a2a_recv,
    rhs_send, near_recv, pass_send, pass_recv, far_recv, ahead_send_sem, ahead_recv_sem,
):
    me = lax.axis_index("xsec")
    row = lax.axis_index("sweep")
    mx, mz, mc = me // 16, (me // 2) % 8, me % 2
    n_faces = cond.shape[1]
    layers = schur.shape[0]
    senders = recv_v.shape[0]
    slots = onehot.shape[2]

    def tile_of(dx):
        return (mx + dx) % NX

    def peer(offset):
        dx, dz, dc = offset
        return tile_of(dx) * 16 + ((mz + dz) % NZ) * 2 + (mc + dc) % 2

    def lanes_of(dx):
        return pl.ds(pl.multiple_of(tile_of(dx) * 128, 128), 128)

    small_copies = [
        pltpu.make_async_copy(source, target, in_sem.at[at])
        for at, (source, target) in enumerate(
            ((inter_h, inter_v), (face_h, face_v), (count_h, count_v), (coup_h, coup_v))
        )
    ]
    cond_copies = [
        pltpu.make_async_copy(
            cond.at[:, :, :, lanes_of(dx)], cond_v.at[:, :, :, lanes_of(dx)], cond_sem.at[at]
        )
        for at, dx in enumerate(DX_ORDER)
    ]

    def schur_copy(layer):
        return pltpu.make_async_copy(schur.at[layer], schur_v.at[layer], schur_sem.at[layer])

    small_copies[0].start()
    cond_copies[0].start()

    order = peers_far_first()
    barrier = pltpu.get_barrier_semaphore()
    for offset in order:
        pl.semaphore_signal(barrier, inc=1, device_id=(row, peer(offset)), device_id_type=MESH)
    pl.semaphore_signal(barrier, inc=1, device_id=((row + 1) % 4, me), device_id_type=MESH)
    pl.semaphore_signal(barrier, inc=1, device_id=((row + 3) % 4, me), device_id_type=MESH)

    for copy in cond_copies[1:] + small_copies[1:] + [schur_copy(layer) for layer in range(layers)]:
        copy.start()

    def send_tile(at):
        dx = DX_ORDER[at]
        for dz in DZ_ORDER:
            for dc in range(2):
                if (dx, dz, dc) == (0, 0, 0):
                    continue
                target = peer((dx, dz, dc))
                pltpu.make_async_remote_copy(
                    src_ref=send_v.at[target], dst_ref=recv_v.at[me],
                    send_sem=a2a_send, recv_sem=a2a_recv.at[at],
                    device_id=(row, target), device_id_type=MESH,
                ).start()

    small_copies[0].wait()
    for at, dx in enumerate(DX_ORDER):
        lanes = lanes_of(dx)
        inter_f[...] = inter_v[:, :, :, lanes].astype(jnp.float32)
        cond_copies[at].wait()

        def one_face(k, carry):
            real = cond_v[0, k, :, lanes].astype(jnp.float32)
            imag = cond_v[1, k, :, lanes].astype(jnp.float32)

            def fold(value):
                return sum(value[8 * v : 8 * v + 8] for v in range(value.shape[0] // 8))

            real_parts = [fold(real * inter_f[0, j] - imag * inter_f[1, j]) for j in range(4)]
            imag_parts = [fold(real * inter_f[1, j] + imag * inter_f[0, j]) for j in range(4)]
            terms[k] = sum_rows(real_parts + imag_parts)
            return carry

        lax.fori_loop(0, n_faces, one_face, 0, unroll=4)
        first = swap_groups([terms[k] for k in range(16)], (8, 4, 2, 1))
        second = swap_groups([terms[k] for k in range(16, 24)], (4, 2, 1))
        base = tile_of(dx) * 16
        left = lane_iota((8, 128)) < 64
        for d in range(16):
            value = second[d % 8]
            if d < 8:
                tail = jnp.where(left, value, pltpu.roll(pltpu.roll(value, 64, 1), 4, 0))
            else:
                tail = jnp.where(left, pltpu.roll(value, 64, 1), pltpu.roll(value, 4, 0))
            send_v[base + d, 0] = first[d][:4].astype(jnp.bfloat16)
            send_v[base + d, 1] = first[d][4:].astype(jnp.bfloat16)
            send_v[base + d, 2] = tail[:4].astype(jnp.bfloat16)
        if at == BARRIER_AT:
            pl.semaphore_wait(barrier, len(order) + 2)
            for earlier in range(at):
                send_tile(earlier)
        if at >= BARRIER_AT:
            send_tile(at)
    recv_v[me] = send_v[me]

    for copy in small_copies[1:]:
        copy.wait()
    n_rows = n_faces * CAP
    index = jnp.concatenate(
        [face_v[...], jnp.zeros((senders, 256 - n_rows), jnp.int32)], 1
    )
    index = jnp.concatenate([index, jnp.zeros((128 - senders, 256), jnp.int32)], 0)
    index = jnp.concatenate([index[:, :128].T, index[:, 128:].T], 0)[:n_rows]
    counts = jnp.concatenate([count_v[...], jnp.zeros((1, 128 - senders), jnp.int32)], 1)
    index = jnp.where(row_iota((n_rows, 128)) % CAP < counts, index, -1)
    index = index.astype(jnp.float32)
    unknown = lane_iota((n_rows, slots)).astype(jnp.float32).astype(jnp.bfloat16)
    one, zero = jnp.ones((), jnp.bfloat16), jnp.zeros((), jnp.bfloat16)

    def some_senders(at, index):
        for c in range(8):
            column = index[:, c : c + 1].astype(jnp.bfloat16)
            onehot[8 * at + c] = jnp.where(column == unknown, one, zero)
        return pltpu.roll(index, 120, 1)

    lax.fori_loop(0, senders // 8, some_senders, index)

    def add_sender(c, total):
        top, bottom, tail = (recv_v[c, part].astype(jnp.float32) for part in range(3))
        head = jnp.concatenate([top, bottom], 0)
        tail = jnp.concatenate([tail[:, :64], tail[:, 64:]], 0)
        block = jnp.concatenate([head, tail], 1).astype(jnp.bfloat16)
        return total + jnp.dot(block, onehot[c], preferred_element_type=jnp.float32)

    loads = jnp.zeros((8, slots), jnp.float32)
    for at, dx in enumerate(DX_ORDER):
        some = recv_v.at[pl.ds(0, 16 if dx else 15)]
        pltpu.make_async_copy(some, some, a2a_recv.at[at]).wait()
        start = tile_of(NX - dx) * 16
        loads = lax.fori_loop(
            0, 16, lambda i, total: add_sender(start + i, total), loads, unroll=8
        )

    sign = jnp.where(row_iota((8, 128)) < 4, -1.0, 1.0)
    groups, far = chips_by_group()
    starts = [sum(len(g) for g in groups[:at]) for at in range(len(groups))]
    near = [chip for group in groups for chip in group]

    def turned(value):
        return sign * pltpu.roll(value, 4, 0)

    def right_side(load, couple, u):
        return load - (couple[0:1] * u + couple[1:2] * turned(u))

    def send_rhs(stage, layer, to_row, own):
        source = rhs_v.at[stage]

        def start(target, dst, sem):
            pltpu.make_async_remote_copy(
                src_ref=source, dst_ref=dst, send_sem=rhs_send.at[stage], recv_sem=sem,
                device_id=(to_row, target), device_id_type=MESH,
            ).start()

        def send_near(chips):
            for chip in chips:
                slot = near.index(opposite(chip))
                group = max(g for g in range(len(groups)) if starts[g] <= slot)
                start(peer((*chip, 0)), near_v.at[layer, slot], near_recv.at[layer, group])

        send_near(groups[-1])
        for chip in reversed(far):
            slot = 2 * far.index(opposite(chip)) + mc
            for dc in range(2):
                start(peer((*chip, dc)), far_v.at[layer, slot], far_recv.at[layer])
        send_near(near[len(near) - len(groups[-1]) - 1 : 0 : -1])

        @pl.when(own)
        def _():
            pltpu.make_async_copy(source, near_v.at[layer, 0], near_recv.at[layer, 0]).start()

        @pl.when(jnp.logical_not(own))
        def _():
            start(me, near_v.at[layer, 0], near_recv.at[layer, 0])

    def passing(layer, group):
        part = pl.ds(starts[group], len(groups[group]))
        return pltpu.make_async_remote_copy(
            src_ref=near_v.at[layer, part], dst_ref=pass_v.at[layer, part],
            send_sem=pass_send.at[layer, group], recv_sem=pass_recv.at[layer, group],
            device_id=(row, peer((0, 0, 1))), device_id_type=MESH,
        )

    def solve(layer):
        passes = []
        schur_copy(layer).wait()
        total = jnp.zeros((8, 256), jnp.float32)

        def rows_of(chip, core):
            first = (tile_of(chip[0]) * 8 + (mz + chip[1]) % NZ) * 256 + core * 128
            rows = pl.ds(pl.multiple_of(first, 128), 128)
            return jnp.concatenate([schur_v[layer, 0, rows, :], schur_v[layer, 1, rows, :]], 1)

        def add_blocks(total, blocks):
            while len(blocks) >= 2:
                pair, blocks = blocks[:2], blocks[2:]
                left = jnp.concatenate([ref[layer, slot] for ref, slot, _, _ in pair], 1)
                right = jnp.concatenate([rows_of(chip, core) for _, _, chip, core in pair], 0)
                total = total + jnp.dot(left, right, preferred_element_type=jnp.float32)
            return total, blocks

        left_over = []
        for at, group in enumerate(groups):
            part = pl.ds(starts[at], len(group))
            some = near_v.at[layer, part]
            pltpu.make_async_copy(some, some, near_recv.at[layer, at]).wait()
            passes.append(passing(layer, at))
            passes[-1].start()
            left_over = left_over + [(near_v, near.index(chip), chip, mc) for chip in group]
        total, left_over = add_blocks(total, left_over)
        def add_passed(total, left_over, at):
            passes[at].wait_recv()
            blocks = [(pass_v, near.index(chip), chip, 1 - mc) for chip in groups[at]]
            return add_blocks(total, left_over + blocks)

        for at in range(len(groups) - 1):
            total, left_over = add_passed(total, left_over, at)
        some = far_v.at[layer]
        pltpu.make_async_copy(some, some, far_recv.at[layer]).wait()
        passes[-1].wait_recv()
        blocks = [(far_v, 2 * at + core, chip, core) for at, chip in enumerate(far) for core in (0, 1)]
        blocks += [(pass_v, near.index(chip), chip, 1 - mc) for chip in groups[-1]]
        total, left_over = add_blocks(total, left_over + blocks)
        assert not left_over
        u = total[:, :128] + turned(total[:, 128:])
        out[layer] = u
        u_v[...] = u

    for layer in range(layers):
        stage_v[layer, 0:8, :] = loads[:, layer * 128 : (layer + 1) * 128]
        stage_v[layer, 8:10, :] = coup_v[layer]
    ahead = pltpu.make_async_remote_copy(
        src_ref=stage_v.at[0], dst_ref=stage_v.at[layers], send_sem=ahead_send_sem,
        recv_sem=ahead_recv_sem, device_id=(row - 1, me), device_id_type=MESH,
    )

    @pl.when(row > 0)
    def _():
        ahead.start()

    u_v[...] = jnp.zeros_like(u_v)

    def one_stage(stage, carry):
        @pl.when(stage > 0)
        def _():
            solve(stage - 1)

        last = stage == layers

        @pl.when(((stage > 0) | (row == 0)) & (jnp.logical_not(last) | (row < 3)))
        def _():
            @pl.when(last)
            def _():
                pltpu.make_async_copy(stage_v.at[0], stage_v.at[layers], ahead_recv_sem).wait()

            rhs = right_side(stage_v[stage, 0:8, :], stage_v[stage, 8:10, :], u_v[...])
            rhs_v[stage] = rhs.astype(jnp.bfloat16)
            send_rhs(stage, stage % layers, row + stage // layers, jnp.logical_not(last))

        return carry

    lax.fori_loop(0, layers + 1, one_stage, 0)

    others = pl.ds(0, senders - 1)
    pltpu.make_async_copy(send_v.at[others], send_v.at[others], a2a_send).wait()
    for layer in range(layers):
        for group in range(len(groups)):
            passing(layer, group).wait_send()

    def wait_sent(stage, count):
        some = near_v.reshape(-1, 8, 128).at[pl.ds(0, count)]
        pltpu.make_async_copy(some, some, rhs_send.at[stage]).wait()

    remote = len(near) - 1 + 2 * len(far)
    wait_sent(1, remote)

    @pl.when(row > 0)
    def _():
        ahead.wait_send()

    @pl.when(row == 0)
    def _():
        wait_sent(0, remote)

    @pl.when(row < 3)
    def _():
        wait_sent(2, remote + 1)


def shards(cond_block, interior_src, face_index, owner_count, coupling, schur_inv):
    cond, inter = cond_block[0, 0], interior_src[0, 0]
    face, count = face_index[0, 0], owner_count[0]
    layers, _, trace, width = schur_inv.shape
    peers = face.shape[0]
    near, far = (sum(map(len, chips_by_group()[0])), len(chips_by_group()[1]))
    vmem = pl.BlockSpec(memory_space=pltpu.VMEM)
    hbm = pl.BlockSpec(memory_space=pl.ANY)
    f32, bf16 = jnp.float32, jnp.bfloat16
    dma = pltpu.SemaphoreType.DMA
    return pl.pallas_call(
        kernel,
        out_shape=pltpu.VMEM((layers, 8, width), f32),
        in_specs=[hbm] * 6,
        out_specs=vmem,
        scratch_shapes=[
            pltpu.VMEM(cond.shape, bf16),
            pltpu.VMEM(schur_inv.shape, bf16),
            pltpu.VMEM(inter.shape, bf16),
            pltpu.VMEM(face.shape, jnp.int32),
            pltpu.VMEM(count.shape, jnp.int32),
            pltpu.VMEM(coupling.shape, f32),
            pltpu.VMEM((*inter.shape[:3], 128), f32),
            pltpu.VMEM((cond.shape[1], 8, 128), f32),
            pltpu.VMEM((peers, 3, 4, 128), bf16),
            pltpu.VMEM((peers, 3, 4, 128), bf16),
            pltpu.VMEM((peers, face.shape[1], layers * width), bf16),
            pltpu.VMEM((layers + 1, 8, width), bf16),
            pltpu.VMEM((layers, near, 8, width), bf16),
            pltpu.VMEM((layers, near, 8, width), bf16),
            pltpu.VMEM((layers, 2 * far, 8, width), bf16),
            pltpu.VMEM((layers + 1, 10, width), f32),
            pltpu.VMEM((8, width), f32),
            dma((4,)), dma((4,)), dma((layers,)), dma, dma((4,)),
            dma((layers + 1,)), dma((layers, len(NEAR))), dma((layers, len(NEAR))),
            dma((layers, len(NEAR))), dma((layers,)), dma, dma,
        ],
        compiler_params=pltpu.CompilerParams(
            collective_id=0, has_side_effects=True, vmem_limit_bytes=VMEM_BYTES
        ),
    )(count, inter, face, coupling, cond, schur_inv)


def solution(mesh):
    placed = (
        P("sweep", "xsec", None, None, None, None),
        P("sweep", "xsec", None, None, None, None),
        P("sweep", "xsec", None, None),
        P("sweep", "xsec", None),
        P("sweep", None, "xsec"),
        P("sweep", None, None, "xsec"),
    )
    return jax.shard_map(
        shards, mesh=mesh, in_specs=placed, out_specs=P("sweep", None, "xsec"), check_vma=False
    )
```
